512 devices in a mesh: pipe: 16 (over y, x_lo), dp: 32 (over z, x_hi, core).
Axes of the slice: x: 4 (x_hi: 2, x_lo: 2; x = x_hi * 2 + x_lo), y: 8, z: 8, core: 2. Of those that a mesh axis runs over, the one named last changes fastest.
Arguments:
- hidden: float32 [256, 2048], P('dp', 'pipe'), may hold values from -6 to 6
- weight: float32 [131072, 2048], P(('pipe', 'dp')), may hold values from -0.375 to 0.375
- log_norm: float32 [256], replicated, may hold values from 14 to 17
- targets: int32 [256], replicated, may hold values from 0 to 131071
- loss_grad: float32 [256], replicated, may hold values from 0.5 to 2
Outputs:
- grad_hidden: float32 [256, 2048], P('dp', 'pipe')
- grad_weight: float32 [131072, 2048], P(('pipe', 'dp'))
The draws below stay inside these ranges and needn't reach their ends.
All inputs are finite; a program needn't handle non-finite values.
Results may differ from the reference program's by a relative error of at most 0.0003.
Values sent between devices are 32-bit elements; how exact they have to be, the bound alone decides.
No kernel may reach another device: no remote copies, remote signals or barrier semaphores. Data moves between devices by JAX's collectives and lax.ppermute only.
A program may use at most 64 MiB of HBM per device.

```python
import jax
import jax.numpy as jnp
from jax import lax

D = 2048
TOKENS = 256
VOCAB = 131072
N_PIPE = 16


def set_ends(drawn, rng, least, largest):
    dims = drawn.shape
    index_at = [jax.random.randint(jax.random.fold_in(rng, axis), (), 0, dims[axis]) for axis in range(len(dims))]
    drawn = drawn.at[tuple(index_at)].set(least)
    longest = dims.index(max(dims))
    index_at[longest] = (index_at[longest] + 1) % dims[longest]
    return drawn.at[tuple(index_at)].set(largest)


def levels(key, dims, shards, smallest, high):
    loudness, own = 1.0, jax.random.fold_in(key, 6)
    for position, parts in shards:
        draws = jnp.exp(jax.random.uniform(jax.random.fold_in(own, position), (parts,), jnp.float32, smallest / len(shards), high / len(shards)))
        loudness = loudness * jnp.repeat(draws, dims[position] // parts).reshape([-1 if axis == position else 1 for axis in range(len(dims))])
    return loudness


def centred(stream_key, extent, scale, limit, pieces=(), kind=jnp.bfloat16):
    entries = scale * jax.random.normal(stream_key, extent, jnp.float32)
    if pieces:
        entries = entries * levels(stream_key, extent, pieces, -0.22, 0.18)
    return jnp.clip(entries, -limit, limit).astype(kind)


def setup_inputs(seed: int = 0) -> dict:
    key_list = jax.random.split(jax.random.key(seed), 6)
    hidden = centred(key_list[0], (TOKENS, D), 1.0, 6.0, ((0, 32), (1, 16)), jnp.float32)
    weight = centred(key_list[1], (VOCAB, D), (D // 9) ** -0.5, 0.375, ((0, 512),), jnp.float32)
    log_norm = jnp.clip(jax.random.uniform(key_list[2], (TOKENS,), jnp.float32, 14.0, 17.0), 14.0, 17.0)
    targets = set_ends(jax.random.randint(key_list[3], (TOKENS,), 0, VOCAB), jax.random.fold_in(key_list[3], 1), 0, VOCAB - 1).astype(jnp.int32)
    loss_grad = jnp.clip(jax.random.uniform(key_list[4], (TOKENS,), jnp.float32, 0.5, 2.0), 0.5, 2.0)
    return {"hidden": hidden, "weight": weight, "log_norm": log_norm, "targets": targets, "loss_grad": loss_grad}


def reference(hidden, weight, log_norm, targets, loss_grad):
    shard_rows = VOCAB // N_PIPE
    tiles = weight.reshape(N_PIPE, shard_rows, D)

    def advance(total, item):
        tile, which = item
        logits = jnp.dot(hidden, tile.T, precision=lax.Precision.HIGHEST, preferred_element_type=jnp.float32)
        prob = jnp.exp(logits - log_norm[:, None])
        columns = which * shard_rows + jnp.arange(shard_rows, dtype=jnp.int32)
        onehot = (targets[:, None] == columns[None, :]).astype(jnp.float32)
        dlogits = loss_grad[:, None] * (prob - onehot)
        total = total + jnp.dot(dlogits, tile, precision=lax.Precision.HIGHEST, preferred_element_type=jnp.float32)
        tile_grad = jnp.dot(dlogits.T, hidden, precision=lax.Precision.HIGHEST, preferred_element_type=jnp.float32)
        return total, tile_grad

    start_total = jnp.zeros((TOKENS, D), jnp.float32)
    grad_hidden, tile_grads = lax.scan(advance, start_total, (tiles, jnp.arange(N_PIPE, dtype=jnp.int32)))
    return grad_hidden, tile_grads.reshape(VOCAB, D)
```

```python
import jax
import jax.numpy as jnp
from jax import lax
from jax.experimental import pallas as pl
from jax.experimental.pallas import tpu as pltpu
from jax.sharding import Mesh
from jax.sharding import PartitionSpec as P

PIPE = ("yh", "yl", "xl")
DP = ("zh", "zl", "xh", "c")
SIZES = (4, 2, 2, 4, 2, 2, 2)
FAR = ("yh", "zh")
NEAR = ("yl", "xl", "zl", "xh")

TOK = 128
ROWS = 256
D = 2048
CHUNK = 512
NCH = D // CHUNK
TILES = (4, 4, 4, 4, 8, 128)


def swap(x):
    return lax.ppermute(x, "c", [(0, 1), (1, 0)])


def spread(block, axes):
    n = lax.axis_size(axes)
    return lax.all_to_all(
        jnp.broadcast_to(block[None], (n, *block.shape)), axes, 0, 0, tiled=True
    )


def parts(a):
    high = a.astype(jnp.bfloat16)
    return high, (a - high.astype(jnp.float32)).astype(jnp.bfloat16)


def dot(a, b, dims):
    return lax.dot_general(a, b, (dims, ((), ())), preferred_element_type=jnp.float32)


def dot3(a, b_high, b_low, dims):
    high, both = a
    m = high.shape[0]
    t = dot(both, b_high, dims)
    return t[:m] + t[m:] + dot(high, b_low, dims)


def columns_of(x_ref, j):
    return jnp.concatenate([x_ref[f, :, j].reshape(TOK, 128) for f in range(4)], axis=1)


def stacked(a):
    high, low = parts(a)
    return high, jnp.concatenate([high, low], axis=0)


def head_kernel(
    first_ref, vec_ref, x_ref, w0, w1, dl_ref, part_ref, wbuf, high, low, sems
):
    copies = {}
    for j in range(NCH):
        cols = pl.ds(j * CHUNK, CHUNK)
        for k, w in ((0, w0), (1, w1)):
            copies[k, j] = pltpu.make_async_copy(
                w.at[:, cols], wbuf.at[k, :, cols], sems.at[k, j]
            )
            copies[k, j].start()
    acc = [jnp.zeros((TOK, ROWS), jnp.float32) for _ in range(2)]
    for j in range(NCH):
        cols = pl.ds(j * CHUNK, CHUNK)
        x = stacked(columns_of(x_ref, j))
        for k in range(2):
            copies[k, j].wait()
            h, l = parts(wbuf[k, :, cols])
            high[k, :, cols] = h
            low[k, :, cols] = l
            acc[k] = acc[k] + dot3(x, h, l, ((1,), (1,)))
    log_norm, grad, target = vec_ref[:, 0:1], vec_ref[:, 1:2], vec_ref[:, 2:3]
    target = target.astype(jnp.int32)
    d = []
    for k in range(2):
        prob = jnp.exp(acc[k] - log_norm)
        column = first_ref[k] + lax.broadcasted_iota(jnp.int32, (TOK, ROWS), 1)
        dl = grad * (prob - (target == column).astype(jnp.float32))
        dl_ref[k] = dl
        d.append(stacked(dl))
    for j in range(NCH):
        cols = pl.ds(j * CHUNK, CHUNK)
        part = dot3(d[0], high[0, :, cols], low[0, :, cols], ((1,), (0,)))
        part += dot3(d[1], high[1, :, cols], low[1, :, cols], ((1,), (0,)))
        for f in range(4):
            part_ref[f, :, j] = part[:, f * 128 : (f + 1) * 128].reshape(4, 4, 8, 128)


def head(first, vec, x, w0, w1):
    vmem = pl.BlockSpec(memory_space=pltpu.VMEM)
    return pl.pallas_call(
        head_kernel,
        out_shape=(
            jax.ShapeDtypeStruct((2, TOK, ROWS), jnp.float32),
            jax.ShapeDtypeStruct(TILES, jnp.float32),
        ),
        in_specs=[
            pl.BlockSpec(memory_space=pltpu.SMEM),
            vmem,
            vmem,
            pl.BlockSpec(memory_space=pltpu.HBM),
            pl.BlockSpec(memory_space=pltpu.HBM),
        ],
        out_specs=(vmem, vmem),
        scratch_shapes=[
            pltpu.VMEM((2, ROWS, D), jnp.float32),
            pltpu.VMEM((2, ROWS, D), jnp.bfloat16),
            pltpu.VMEM((2, ROWS, D), jnp.bfloat16),
            pltpu.SemaphoreType.DMA((2, NCH)),
        ],
        compiler_params=pltpu.CompilerParams(vmem_limit_bytes=24 << 20),
        cost_estimate=pl.CostEstimate(
            flops=12 * TOK * ROWS * D * 2,
            bytes_accessed=6 << 20,
            transcendentals=2 * TOK * ROWS,
        ),
        name="head",
    )(first, vec, x, w0, w1)


def weight_grad_kernel(d0_ref, d1_ref, x0_ref, x1_ref, out_ref):
    d = jnp.concatenate([d0_ref[...].T, d1_ref[...].T], axis=1)
    d = stacked(d)
    for j in range(NCH):
        x = jnp.concatenate([columns_of(x0_ref, j), columns_of(x1_ref, j)], axis=0)
        out_ref[:, pl.ds(j * CHUNK, CHUNK)] = dot3(d, *parts(x), ((1,), (0,)))


def weight_grad(d0, d1, x0, x1):
    vmem = pl.BlockSpec(memory_space=pltpu.VMEM)
    return pl.pallas_call(
        weight_grad_kernel,
        out_shape=jax.ShapeDtypeStruct((ROWS, D), jnp.float32),
        in_specs=[vmem] * 4,
        out_specs=vmem,
        compiler_params=pltpu.CompilerParams(vmem_limit_bytes=24 << 20),
        cost_estimate=pl.CostEstimate(
            flops=6 * 2 * TOK * ROWS * D, bytes_accessed=5 << 20, transcendentals=0
        ),
        name="weight_grad",
    )(d0, d1, x0, x1)


def sum_kernel(x_ref, out_ref):
    total = x_ref[0]
    for i in range(1, x_ref.shape[0]):
        total = total + x_ref[i]
    out_ref[...] = total


def local_sum(x):
    vmem = pl.BlockSpec(memory_space=pltpu.VMEM)
    return pl.pallas_call(
        sum_kernel,
        out_shape=jax.ShapeDtypeStruct(x.shape[1:], jnp.float32),
        in_specs=[vmem],
        out_specs=vmem,
        compiler_params=pltpu.CompilerParams(vmem_limit_bytes=8 << 20),
        name="local_sum",
    )(x)


def on_device(hidden, weight, log_norm, targets, loss_grad):
    c = lax.axis_index("c")
    shard = lax.axis_index(PIPE + DP)
    far = spread(hidden, FAR)
    own_weight, far = lax.optimization_barrier((weight, far))
    other_weight = swap(own_weight)
    near = spread(far, NEAR).reshape(TILES)

    vec = jnp.stack([log_norm, loss_grad, targets.astype(jnp.float32)], axis=1)
    vec = vec.reshape(4, 2, 2, 2, 8, 3)
    vec = lax.dynamic_index_in_dim(vec, c, axis=3, keepdims=False)
    vec = vec.transpose(1, 2, 0, 3, 4).reshape(TOK, 3)
    first = jnp.stack([shard, shard + 1 - 2 * c]).astype(jnp.int32) * ROWS

    dl, part = head(first, vec, near, weight, other_weight)

    got = lax.all_to_all(part.reshape(16, 16, 8, 128), NEAR, 0, 0, tiled=True)
    got = lax.all_to_all(local_sum(got), FAR, 0, 0, tiled=True)
    got = local_sum(got)

    near, dl = lax.optimization_barrier((near, dl))
    grad_weight = weight_grad(dl[0], swap(dl[1]), near, swap(near))
    return (got, grad_weight)


def solution(mesh):
    fine = Mesh(mesh.devices.reshape(SIZES), PIPE + DP)
    in_specs = (P(DP, PIPE), P(PIPE + DP, None), P(), P(), P())
    out_specs = (P(DP, PIPE), P(PIPE + DP, None))
    return jax.shard_map(
        on_device, mesh=fine, in_specs=in_specs, out_specs=out_specs, check_vma=False
    )
```

```python
import jax
import jax.numpy as jnp
from jax import lax
from jax.experimental import pallas as pl
from jax.experimental.pallas import tpu as pltpu
from jax.sharding import Mesh
from jax.sharding import PartitionSpec as P

PIPE = ("yh", "yl", "xl")
DP = ("zh", "zl", "xh", "c")
SIZES = (4, 2, 2, 4, 2, 2, 2)


def device(y, x, z, c):
    return y * 64 + x % 2 * 32 + z * 4 + x // 2 * 2 + c


def pairs(n, c):
    return [((i + 2 * c) % n, i + 1) for i in range(0, n, 2)]


FAR = [
    [
        device(2 * yh + yl, 2 * xh + xl, 2 * zh + zl, c)
        for yh in range(4)
        for zh in range(4)
        for xh in range(2)
    ]
    for c in range(2)
    for yl in range(2)
    for xl in range(2)
    for zl in range(2)
]
NEAR = [
    [device(y, x, z, c) for y in ys for x in xs for z in zs]
    for c in range(2)
    for ys in pairs(8, c)
    for xs in pairs(4, c)
    for zs in pairs(8, c)
]

TOK = 128
ROWS = 256
D = 2048
CHUNK = 512
SPLIT_VMEM, HEAD_VMEM = 62, 50
PIECES = 4
NCH = D // CHUNK
TILES = (4, 2, 4, 8, 8, 128)


def swap(x):
    return lax.ppermute(x, "c", [(0, 1), (1, 0)])


def exchange(x, groups):
    return lax.all_to_all(
        x, PIPE + DP, 0, 0, axis_index_groups=groups, tiled=True
    )


def spread(block, groups):
    n = len(groups[0])
    return exchange(jnp.broadcast_to(block[None], (n, *block.shape)), groups)


def parts(a):
    high = a.astype(jnp.bfloat16)
    return high, (a - high.astype(jnp.float32)).astype(jnp.bfloat16)


def dot(a, b, dims):
    return lax.dot_general(a, b, (dims, ((), ())), preferred_element_type=jnp.float32)


def dot3(a, b_high, b_low, dims):
    high, both = a
    m = high.shape[0]
    t = dot(both, b_high, dims)
    return t[:m] + t[m:] + dot(high, b_low, dims)


def columns_of(x_ref, j):
    return jnp.concatenate([x_ref[f, :, j].reshape(TOK, 128) for f in range(4)], axis=1)


def stacked(a):
    high, low = parts(a)
    return high, jnp.concatenate([high, low], axis=0)


def split_kernel(w0_ref, w1_ref, high_ref, low_ref):
    for k, w in ((0, w0_ref), (1, w1_ref)):
        rows = pl.ds(k * ROWS, ROWS)
        high_ref[rows], low_ref[rows] = parts(w[...])


def split(w0, w1):
    vmem = pl.BlockSpec(memory_space=pltpu.VMEM)
    out = jax.ShapeDtypeStruct((2 * ROWS, D), jnp.bfloat16)
    return pl.pallas_call(
        split_kernel,
        out_shape=(out, out),
        in_specs=[vmem, vmem],
        out_specs=(vmem, vmem),
        compiler_params=pltpu.CompilerParams(vmem_limit_bytes=SPLIT_VMEM << 20),
        cost_estimate=pl.CostEstimate(
            flops=6 * ROWS * D, bytes_accessed=8 << 20, transcendentals=0
        ),
        name="split",
    )(w0, w1)


def head_kernel(
    first_ref,
    vec_ref,
    x_ref,
    high_ref,
    low_ref,
    dl0_ref,
    dl1_ref,
    part_ref,
    high,
    low,
    xs,
    out,
    ins,
    outs,
):
    fetches = []
    for p, (src, dst) in enumerate(((high_ref, high), (low_ref, low))):
        for i in range(PIECES):
            rows = pl.ds(i * (2 * ROWS // PIECES), 2 * ROWS // PIECES)
            fetches.append(
                pltpu.make_async_copy(src.at[rows], dst.at[rows], ins.at[p, i])
            )
            fetches[-1].start()
    for j in range(NCH):
        for f in range(4):
            cols = pl.ds(j * CHUNK + f * 128, 128)
            xs[:TOK, cols], xs[TOK:, cols] = parts(x_ref[f, :, j].reshape(TOK, 128))
    for fetch in fetches[:PIECES]:
        fetch.wait()
    both = dot(xs[...], high[...], ((1,), (1,)))
    for fetch in fetches[PIECES:]:
        fetch.wait()
    logits = both[:TOK] + both[TOK:] + dot(xs[:TOK], low[...], ((1,), (1,)))
    log_norm, grad, target = vec_ref[:, 0:1], vec_ref[:, 1:2], vec_ref[:, 2:3]
    target = target.astype(jnp.int32)
    d = []
    for k, dl_ref in ((0, dl0_ref), (1, dl1_ref)):
        prob = jnp.exp(logits[:, k * ROWS : (k + 1) * ROWS] - log_norm)
        column = first_ref[k] + lax.broadcasted_iota(jnp.int32, (TOK, ROWS), 1)
        dl = grad * (prob - (target == column).astype(jnp.float32))
        dl_ref[...] = dl
        d.append(stacked(dl))
    copies = []
    for j in range(NCH):
        cols = pl.ds(j * CHUNK, CHUNK)
        part = dot3(d[0], high[:ROWS, cols], low[:ROWS, cols], ((1,), (0,)))
        part += dot3(d[1], high[ROWS:, cols], low[ROWS:, cols], ((1,), (0,)))
        for f in range(4):
            out[j, f] = part[:, f * 128 : (f + 1) * 128].reshape(2, 8, 8, 128)
            copies.append(
                pltpu.make_async_copy(out.at[j, f], part_ref.at[f, :, j], outs.at[j, f])
            )
            copies[-1].start()
    for copy in copies:
        copy.wait()


def head(first, vec, x, high, low):
    vmem = pl.BlockSpec(memory_space=pltpu.VMEM)
    hbm = pl.BlockSpec(memory_space=pl.ANY)
    dl = jax.ShapeDtypeStruct((TOK, ROWS), jnp.float32)
    return pl.pallas_call(
        head_kernel,
        out_shape=(dl, dl, jax.ShapeDtypeStruct(TILES, jnp.float32)),
        in_specs=[pl.BlockSpec(memory_space=pltpu.SMEM), vmem, vmem, hbm, hbm],
        out_specs=(vmem, vmem, hbm),
        scratch_shapes=[
            pltpu.VMEM((2 * ROWS, D), jnp.bfloat16),
            pltpu.VMEM((2 * ROWS, D), jnp.bfloat16),
            pltpu.VMEM((2 * TOK, D), jnp.bfloat16),
            pltpu.VMEM((NCH, 4, 2, 8, 8, 128), jnp.float32),
            pltpu.SemaphoreType.DMA((2, PIECES)),
            pltpu.SemaphoreType.DMA((NCH, 4)),
        ],
        compiler_params=pltpu.CompilerParams(vmem_limit_bytes=HEAD_VMEM << 20),
        cost_estimate=pl.CostEstimate(
            flops=12 * TOK * ROWS * D * 2,
            bytes_accessed=6 << 20,
            transcendentals=2 * TOK * ROWS,
        ),
        name="head",
    )(first, vec, x, high, low)


def weight_grad_kernel(d0_ref, d1_ref, x0_ref, x1_ref, out_ref):
    d = jnp.concatenate([d0_ref[...].T, d1_ref[...].T], axis=1)
    d = stacked(d)
    for j in range(NCH):
        x = jnp.concatenate([columns_of(x0_ref, j), columns_of(x1_ref, j)], axis=0)
        out_ref[:, pl.ds(j * CHUNK, CHUNK)] = dot3(d, *parts(x), ((1,), (0,)))


def weight_grad(d0, d1, x0, x1):
    vmem = pl.BlockSpec(memory_space=pltpu.VMEM)
    return pl.pallas_call(
        weight_grad_kernel,
        out_shape=jax.ShapeDtypeStruct((ROWS, D), jnp.float32),
        in_specs=[vmem] * 4,
        out_specs=vmem,
        compiler_params=pltpu.CompilerParams(vmem_limit_bytes=24 << 20),
        cost_estimate=pl.CostEstimate(
            flops=6 * 2 * TOK * ROWS * D, bytes_accessed=5 << 20, transcendentals=0
        ),
        name="weight_grad",
    )(d0, d1, x0, x1)


def sum_kernel(x_ref, out_ref):
    total = x_ref[0]
    for i in range(1, x_ref.shape[0]):
        total = total + x_ref[i]
    out_ref[...] = total


def local_sum(x):
    vmem = pl.BlockSpec(memory_space=pltpu.VMEM)
    return pl.pallas_call(
        sum_kernel,
        out_shape=jax.ShapeDtypeStruct(x.shape[1:], jnp.float32),
        in_specs=[vmem],
        out_specs=vmem,
        compiler_params=pltpu.CompilerParams(vmem_limit_bytes=8 << 20),
        name="local_sum",
    )(x)


def on_device(hidden, weight, log_norm, targets, loss_grad):
    c = lax.axis_index("c")
    shard = lax.axis_index(PIPE + DP)

    vec = jnp.stack([log_norm, loss_grad, targets.astype(jnp.float32)], axis=1)
    vec = vec.reshape(4, 2, 2, 2, 8, 3)
    vec = lax.dynamic_index_in_dim(vec, c, axis=3, keepdims=False)
    vec = vec.transpose(1, 0, 2, 3, 4).reshape(TOK, 3)
    first = jnp.stack([shard, shard + 1 - 2 * c]).astype(jnp.int32) * ROWS

    far = spread(hidden, FAR)
    other_weight = swap(weight)
    near = spread(far, NEAR).reshape(TILES)
    high, low = split(weight, other_weight)
    dl0, dl1, part = head(first, vec, near, high, low)
    got = part.reshape(8, 32, 8, 128)
    got = exchange(got, NEAR)
    got = local_sum(got)
    got = exchange(got, FAR)
    got = local_sum(got)
    other_near = swap(near)
    other_dl = swap(dl1)
    grad_weight = weight_grad(dl0, other_dl, near, other_near)
    return (got, grad_weight)


def solution(mesh):
    fine = Mesh(mesh.devices.reshape(SIZES), PIPE + DP)
    in_specs = (P(DP, PIPE), P(PIPE + DP, None), P(), P(), P())
    out_specs = (P(DP, PIPE), P(PIPE + DP, None))
    return jax.shard_map(
        on_device, mesh=fine, in_specs=in_specs, out_specs=out_specs, check_vma=False
    )
```

```python
import jax
import jax.numpy as jnp
from jax import lax
from jax.experimental import pallas as pl
from jax.experimental.pallas import tpu as pltpu
from jax.sharding import Mesh
from jax.sharding import PartitionSpec as P

PIPE = ("yh", "yl", "xl")
DP = ("zh", "zl", "xh", "c")
SIZES = (4, 2, 2, 4, 2, 2, 2)


def device(y, x, z, c):
    return y * 64 + x % 2 * 32 + z * 4 + x // 2 * 2 + c


def pairs(n, c):
    return [((i + 2 * c) % n, i + 1) for i in range(0, n, 2)]


FAR = [
    [
        device(2 * yh + yl, 2 * xh + xl, 2 * zh + zl, c)
        for yh in range(4)
        for zh in range(4)
        for xh in range(2)
    ]
    for c in range(2)
    for yl in range(2)
    for xl in range(2)
    for zl in range(2)
]
NEAR = [
    [device(y, x, z, c) for y in ys for x in xs for z in zs]
    for c in range(2)
    for ys in pairs(8, c)
    for xs in pairs(4, c)
    for zs in pairs(8, c)
]

TOK = 128
ROWS = 256
D = 2048
CHUNK = 512
HEAD_VMEM = 50
PIECES = 2
NCH = D // CHUNK
TILES = (4, 2, 4, 8, 8, 128)


def swap(x):
    return lax.ppermute(x, "c", [(0, 1), (1, 0)])


def exchange(x, groups):
    return lax.all_to_all(
        x, PIPE + DP, 0, 0, axis_index_groups=groups, tiled=True
    )


def spread(block, groups):
    n = len(groups[0])
    return exchange(jnp.broadcast_to(block[None], (n, *block.shape)), groups)


def parts(a):
    high = a.astype(jnp.bfloat16)
    return high, (a - high.astype(jnp.float32)).astype(jnp.bfloat16)


def dot(a, b, dims):
    return lax.dot_general(a, b, (dims, ((), ())), preferred_element_type=jnp.float32)


def dot3(a, b_high, b_low, dims):
    high, both = a
    m = high.shape[0]
    t = dot(both, b_high, dims)
    return t[:m] + t[m:] + dot(high, b_low, dims)


def columns_of(x_ref, j):
    return jnp.concatenate([x_ref[f, :, j].reshape(TOK, 128) for f in range(4)], axis=1)


def stacked(a):
    high, low = parts(a)
    return high, jnp.concatenate([high, low], axis=0)


def head_kernel(
    first_ref,
    vec_ref,
    x_ref,
    w0_ref,
    w1_ref,
    dl0_ref,
    dl1_ref,
    part_ref,
    w,
    high,
    low,
    xs,
    out,
    ins,
    outs,
):
    fetches = []
    n = ROWS // PIECES
    for k, src in enumerate((w0_ref, w1_ref)):
        for i in range(PIECES):
            fetches.append(
                pltpu.make_async_copy(
                    src.at[pl.ds(i * n, n)],
                    w.at[pl.ds(k * ROWS + i * n, n)],
                    ins.at[k, i],
                )
            )
            fetches[-1].start()
    for j in range(NCH):
        for f in range(4):
            cols = pl.ds(j * CHUNK + f * 128, 128)
            xs[:TOK, cols], xs[TOK:, cols] = parts(x_ref[f, :, j].reshape(TOK, 128))
    for i, fetch in enumerate(fetches):
        fetch.wait()
        rows = pl.ds(i * n, n)
        high[rows], low[rows] = parts(w[rows])
    both = dot(xs[...], high[...], ((1,), (1,)))
    logits = both[:TOK] + both[TOK:] + dot(xs[:TOK], low[...], ((1,), (1,)))
    log_norm, grad, target = vec_ref[:, 0:1], vec_ref[:, 1:2], vec_ref[:, 2:3]
    target = target.astype(jnp.int32)
    d = []
    for k, dl_ref in ((0, dl0_ref), (1, dl1_ref)):
        prob = jnp.exp(logits[:, k * ROWS : (k + 1) * ROWS] - log_norm)
        column = first_ref[k] + lax.broadcasted_iota(jnp.int32, (TOK, ROWS), 1)
        dl = grad * (prob - (target == column).astype(jnp.float32))
        dl_ref[...] = dl
        d.append(stacked(dl))
    copies = []
    for j in range(NCH):
        cols = pl.ds(j * CHUNK, CHUNK)
        part = dot3(d[0], high[:ROWS, cols], low[:ROWS, cols], ((1,), (0,)))
        part += dot3(d[1], high[ROWS:, cols], low[ROWS:, cols], ((1,), (0,)))
        for f in range(4):
            out[j, f] = part[:, f * 128 : (f + 1) * 128].reshape(2, 8, 8, 128)
            copies.append(
                pltpu.make_async_copy(out.at[j, f], part_ref.at[f, :, j], outs.at[j, f])
            )
            copies[-1].start()
    for copy in copies:
        copy.wait()


def head(first, vec, x, w0, w1):
    vmem = pl.BlockSpec(memory_space=pltpu.VMEM)
    hbm = pl.BlockSpec(memory_space=pl.ANY)
    dl = jax.ShapeDtypeStruct((TOK, ROWS), jnp.float32)
    return pl.pallas_call(
        head_kernel,
        out_shape=(dl, dl, jax.ShapeDtypeStruct(TILES, jnp.float32)),
        in_specs=[pl.BlockSpec(memory_space=pltpu.SMEM), vmem, vmem, hbm, hbm],
        out_specs=(vmem, vmem, hbm),
        scratch_shapes=[
            pltpu.VMEM((2 * ROWS, D), jnp.float32),
            pltpu.VMEM((2 * ROWS, D), jnp.bfloat16),
            pltpu.VMEM((2 * ROWS, D), jnp.bfloat16),
            pltpu.VMEM((2 * TOK, D), jnp.bfloat16),
            pltpu.VMEM((NCH, 4, 2, 8, 8, 128), jnp.float32),
            pltpu.SemaphoreType.DMA((2, PIECES)),
            pltpu.SemaphoreType.DMA((NCH, 4)),
        ],
        compiler_params=pltpu.CompilerParams(vmem_limit_bytes=HEAD_VMEM << 20),
        cost_estimate=pl.CostEstimate(
            flops=12 * TOK * ROWS * D * 2,
            bytes_accessed=6 << 20,
            transcendentals=2 * TOK * ROWS,
        ),
        name="head",
    )(first, vec, x, w0, w1)


def weight_grad_kernel(d0_ref, d1_ref, x0_ref, x1_ref, out_ref):
    d = jnp.concatenate([d0_ref[...].T, d1_ref[...].T], axis=1)
    d = stacked(d)
    for j in range(NCH):
        x = jnp.concatenate([columns_of(x0_ref, j), columns_of(x1_ref, j)], axis=0)
        out_ref[:, pl.ds(j * CHUNK, CHUNK)] = dot3(d, *parts(x), ((1,), (0,)))


def weight_grad(d0, d1, x0, x1):
    vmem = pl.BlockSpec(memory_space=pltpu.VMEM)
    return pl.pallas_call(
        weight_grad_kernel,
        out_shape=jax.ShapeDtypeStruct((ROWS, D), jnp.float32),
        in_specs=[vmem] * 4,
        out_specs=vmem,
        compiler_params=pltpu.CompilerParams(vmem_limit_bytes=24 << 20),
        cost_estimate=pl.CostEstimate(
            flops=6 * 2 * TOK * ROWS * D, bytes_accessed=5 << 20, transcendentals=0
        ),
        name="weight_grad",
    )(d0, d1, x0, x1)


def sum_kernel(x_ref, out_ref):
    total = x_ref[0]
    for i in range(1, x_ref.shape[0]):
        total = total + x_ref[i]
    out_ref[...] = total


def local_sum(x):
    vmem = pl.BlockSpec(memory_space=pltpu.VMEM)
    return pl.pallas_call(
        sum_kernel,
        out_shape=jax.ShapeDtypeStruct(x.shape[1:], jnp.float32),
        in_specs=[vmem],
        out_specs=vmem,
        compiler_params=pltpu.CompilerParams(vmem_limit_bytes=8 << 20),
        name="local_sum",
    )(x)


def on_device(hidden, weight, log_norm, targets, loss_grad):
    c = lax.axis_index("c")
    shard = lax.axis_index(PIPE + DP)

    vec = jnp.stack([log_norm, loss_grad, targets.astype(jnp.float32)], axis=1)
    vec = vec.reshape(4, 2, 2, 2, 8, 3)
    vec = lax.dynamic_index_in_dim(vec, c, axis=3, keepdims=False)
    vec = vec.transpose(1, 0, 2, 3, 4).reshape(TOK, 3)
    first = jnp.stack([shard, shard + 1 - 2 * c]).astype(jnp.int32) * ROWS

    far = spread(hidden, FAR)
    own_weight, far = lax.optimization_barrier((weight, far))
    other_weight = swap(own_weight)
    near = spread(far, NEAR).reshape(TILES)
    dl0, dl1, part = head(first, vec, near, own_weight, other_weight)
    got = part.reshape(8, 32, 8, 128)
    got = exchange(got, NEAR)
    got = local_sum(got)
    got = exchange(got, FAR)
    got = local_sum(got)
    other_near = swap(near)
    other_dl = swap(dl1)
    grad_weight = weight_grad(dl0, other_dl, near, other_near)
    return (got, grad_weight)


def solution(mesh):
    fine = Mesh(mesh.devices.reshape(SIZES), PIPE + DP)
    in_specs = (P(DP, PIPE), P(PIPE + DP, None), P(), P(), P())
    out_specs = (P(DP, PIPE), P(PIPE + DP, None))
    return jax.shard_map(
        on_device, mesh=fine, in_specs=in_specs, out_specs=out_specs, check_vma=False
    )
```
